32 devices in a mesh: groups: 2 (over y), passage: 8 (over z, x), tensor: 2 (over core).
Axes of the slice: x: 2, y: 2, z: 4, core: 2. Of those that a mesh axis runs over, the one named last changes fastest.
Arguments:
- corpus: bfloat16 [96, 256, 1024], P(('groups', 'passage')), parts along dimension 0, may hold values from -6 to 6
- queries: bfloat16 [32, 2048], P(('groups', 'passage'), 'tensor'), parts along dimension 0, may hold values from -180 to 180
- key_weight: bfloat16 [1024, 2048], P('passage', 'tensor'), may hold values from -0.1875 to 0.1875
- value_weight: bfloat16 [1024, 2048], P('passage', 'tensor'), may hold values from -0.1875 to 0.1875
- retrieved: int32 [2, 16], P('groups'), parts along dimension 0, may hold values from 0 to 47, as said below
- placement_map: int32 [96], P('groups'), parts along dimension 0, may hold values from 0 to 47, as said below
- valid_counts: int32 [96], P('groups'), parts along dimension 0, may hold values from 16 to 256
Outputs:
- context: bfloat16 [32, 2048], P(('groups', 'passage'), 'tensor'), parts along dimension 0
The draws below stay inside these ranges and needn't reach their ends.
There are 2 independent parts, one for each index of `groups`. The reference program is written for one: setup_inputs(seed, part) draws one part's arguments, and reference() takes and returns one part's arrays. A program takes and returns all parts, laid end to end along the dimension named above; an argument that names none is the same for every part. Nothing has to cross between parts.
Inputs may be any that keep to these rules, and one draw needn't show every extreme that they name: Each row lists 16 ids; all 16 retrieved ids are distinct. With shard = placement_map[id] // 6, at most 5 retrieved passages lie on one shard, and some shard holds exactly 5. `placement_map`: A permutation of the corpus rows.
All inputs are finite; a program needn't handle non-finite values.
Results may differ from the reference program's by a relative error of at most 0.01.
The reference program's roundings to bfloat16 on the way (of `normed`, `key_rows` and `weights`) count: a program that leaves them out, or rounds other values in their place, can miss the bound.
Values may be sent and summed in bfloat16 or wider, within the bound.
A program may use at most 64 MiB of HBM per device.

```python
import jax
import jax.numpy as jnp
from jax import lax

DE = 1024
H = 32
DH = 64
LEN = 256
PER_Q = 16
MOST = 5
CORP_DEV = 6
QT = 16
Q = 1
RET = 16
QROWS = 16
NCORP = 48
HD = 2048


def draw_placement_map(key, part):
    return jax.random.permutation(jax.random.fold_in(key, 11), NCORP).astype(jnp.int32)


def draw_retrieved(key, part):
    layout = jax.random.permutation(jax.random.fold_in(key, 11), NCORP).astype(jnp.int32)
    inverse = jnp.argsort(layout, stable=True).astype(jnp.int32)
    shards = NCORP // CORP_DEV
    capacity = shards * MOST
    busiest = jax.random.randint(jax.random.fold_in(key, 12), (), 0, shards)
    shuffled = jax.random.permutation(jax.random.fold_in(key, 13), capacity).astype(jnp.int32)
    slot_shard = jnp.arange(capacity, dtype=jnp.int32) // MOST
    slot_number = jnp.arange(capacity, dtype=jnp.int32) % MOST
    ordering = jnp.where(slot_shard == busiest, slot_number - MOST, shuffled)
    chosen = jnp.argsort(ordering, stable=True)[:RET]
    offsets = jax.random.randint(jax.random.fold_in(key, 14), (shards,), 0, CORP_DEV)
    local_row = (slot_number[chosen] + offsets[slot_shard[chosen]]) % CORP_DEV
    corpus_row = slot_shard[chosen] * CORP_DEV + local_row
    reorder = jax.random.permutation(jax.random.fold_in(key, 15), RET)
    corpus_row = corpus_row[reorder]
    return inverse[corpus_row].reshape(Q, PER_Q).astype(jnp.int32)


def draw_valid_counts(key, part):
    lowest = max(1, LEN // 16)
    counts = jax.random.randint(jax.random.fold_in(key, 21), (NCORP,), lowest, LEN + LEN // 2)
    counts = jnp.minimum(counts, LEN)
    chosen = jax.random.randint(jax.random.fold_in(key, 22), (), 0, NCORP)
    return counts.at[chosen].set(LEN).astype(jnp.int32)


def draw_queries(key, part):
    values = jnp.clip(2.5 * jax.random.normal(jax.random.fold_in(key, 31), (QROWS, H * DH), jnp.float32), -10.0, 10.0)
    return values.astype(jnp.bfloat16)


def steps_of(key, extent, split, low, top_value):
    gain, own = 1.0, jax.random.fold_in(key, 6)
    for axis_at, blocks in split:
        draws = jnp.exp(jax.random.uniform(jax.random.fold_in(own, axis_at), (blocks,), jnp.float32, low / len(split), top_value / len(split)))
        gain = gain * jnp.repeat(draws, extent[axis_at] // blocks).reshape([-1 if axis == axis_at else 1 for axis in range(len(extent))])
    return gain


def bell_draw(own_key, dims, width, bound, cuts=(), held_as=jnp.bfloat16):
    values = width * jax.random.normal(own_key, dims, jnp.float32)
    if cuts:
        values = values * steps_of(own_key, dims, cuts, -0.22, 0.18)
    return jnp.clip(values, -bound, bound).astype(held_as)


def setup_inputs(seed: int = 0, part: int = 0) -> dict:
    splits = jax.random.split(jax.random.key(seed), 8)
    part_splits = jax.random.split(jax.random.fold_in(splits[7], part), 8)
    corpus = bell_draw(part_splits[0], (NCORP, LEN, DE), 1.0, 6.0, ((0, 8),))
    queries = draw_queries(jax.random.fold_in(jax.random.fold_in(splits[7], part), 71), part)
    key_weight = bell_draw(splits[2], (DE, HD), DE ** -0.5, 0.1875, ((0, 8), (1, 2)))
    value_weight = bell_draw(splits[3], (DE, HD), DE ** -0.5, 0.1875, ((0, 8), (1, 2)))
    retrieved = draw_retrieved(jax.random.fold_in(jax.random.fold_in(splits[7], part), 71), part)
    placement_map = draw_placement_map(jax.random.fold_in(jax.random.fold_in(splits[7], part), 71), part)
    valid_counts = draw_valid_counts(jax.random.fold_in(jax.random.fold_in(splits[7], part), 71), part)
    return dict(corpus=corpus, queries=queries, key_weight=key_weight, value_weight=value_weight, retrieved=retrieved, placement_map=placement_map, valid_counts=valid_counts)


def normalize(hidden):
    values32 = hidden.astype(jnp.float32)
    factor = lax.rsqrt(lax.optimization_barrier(jnp.mean(values32 * values32, axis=-1, keepdims=True)) + 1e-06)
    return (values32 * factor).astype(jnp.bfloat16)

def reference(corpus, queries, key_weight, value_weight, retrieved, placement_map, valid_counts):
    heads = key_weight.shape[1] // DH
    corpus_rows = placement_map[retrieved].astype(jnp.int32)
    lengths = valid_counts[retrieved].astype(jnp.int32)
    query_blocks = queries.reshape(Q, QT, heads, DH).astype(jnp.float32)
    positions = jnp.arange(LEN, dtype=jnp.int32)
    scaling = DH ** (-0.5)

    def per_passage(block, inputs):
        corpus_row, length_now = inputs
        tokens = lax.dynamic_index_in_dim(corpus, corpus_row, 0, keepdims=False)
        normed = normalize(tokens)
        key_rows = jnp.dot(normed, key_weight, preferred_element_type=jnp.float32).astype(jnp.bfloat16)
        value_rows = jnp.dot(normed, value_weight, preferred_element_type=jnp.float32).astype(jnp.bfloat16)
        key_rows = key_rows.reshape(LEN, heads, DH).astype(jnp.float32)
        value_rows = value_rows.reshape(LEN, heads, DH).astype(jnp.float32)
        scores = jnp.einsum('thd,lhd->htl', block, key_rows) * scaling
        live_mask = (positions < length_now)[None, None, :]
        scores = jnp.where(live_mask, scores, jnp.float32(-1e+30))
        top_score = lax.optimization_barrier(jnp.max(scores, axis=-1))
        weights = jnp.where(live_mask, jnp.exp(scores - top_score[..., None]), jnp.float32(0.0))
        row_mass = lax.optimization_barrier(jnp.sum(weights, axis=-1))
        rounded = weights.astype(jnp.bfloat16).astype(jnp.float32)
        partial_ctx = jnp.einsum('htl,lhd->htd', rounded, value_rows)
        return (block, (top_score, row_mass, partial_ctx))

    def per_question(inputs):
        block, row_list, length_list = inputs
        _, (tops, masses, parts) = lax.scan(per_passage, block, (row_list, length_list))
        peak = lax.optimization_barrier(jnp.max(tops, axis=0))
        factor = jnp.exp(tops - peak[None])
        numer = lax.optimization_barrier(jnp.sum(factor[..., None] * parts, axis=0))
        denom = lax.optimization_barrier(jnp.sum(factor * masses, axis=0))
        context = numer / denom[..., None]
        return jnp.transpose(context, (1, 0, 2)).reshape(QT, heads * DH)
    result = lax.map(per_question, (query_blocks, corpus_rows, lengths))
    return result.reshape(QROWS, heads * DH).astype(jnp.bfloat16)
```

```python
import jax
import jax.numpy as jnp
from jax import lax
from jax.experimental import pallas as pl
from jax.experimental.pallas import tpu as pltpu
from jax.sharding import PartitionSpec as P

DH = 64
LEN = 256
MOST = 5
QT = 16


def normalize(hidden):
    values32 = hidden.astype(jnp.float32)
    factor = lax.rsqrt(jnp.mean(values32 * values32, axis=-1, keepdims=True) + 1e-06)
    return (values32 * factor).astype(jnp.bfloat16)


def widen(stats):
    return jnp.repeat(stats, DH, axis=-1)


def join_partials(first, second):
    top_one, mass_one, ctx_one = first
    top_two, mass_two, ctx_two = second
    highest = jnp.maximum(top_one, top_two)
    scale_one = jnp.exp(top_one - highest)
    scale_two = jnp.exp(top_two - highest)
    return (
        highest,
        mass_one * scale_one + mass_two * scale_two,
        ctx_one * widen(scale_one) + ctx_two * widen(scale_two),
    )


def on_device(corpus, queries, key_weight, value_weight, retrieved, placement_map, valid_counts):
    shard_index = lax.axis_index("passage")
    corp_rows = corpus.shape[0]
    per_question = retrieved.shape[1]
    total_ret = retrieved.shape[0] * per_question
    flat_ids = retrieved.reshape(total_ret)
    corpus_row = placement_map[flat_ids]
    lengths = valid_counts[flat_ids]
    owned_mask = corpus_row // corp_rows == shard_index
    owner_rank = jnp.cumsum(owned_mask.astype(jnp.int32)) - 1
    slot_iota = jnp.arange(MOST, dtype=jnp.int32)
    selector = (owned_mask[None, :] & (owner_rank[None, :] == slot_iota[:, None])).astype(jnp.int32)
    local_rows = jnp.sum(selector * (corpus_row % corp_rows)[None, :], axis=1)
    slot_lengths = jnp.sum(selector * lengths[None, :], axis=1)
    question_ids = jnp.arange(total_ret, dtype=jnp.int32) // per_question
    slot_question = jnp.sum(selector * question_ids[None, :], axis=1)
    passages = corpus[local_rows]
    normed = normalize(passages).reshape(MOST * LEN, passages.shape[2])
    full_key, full_value = (
        lax.all_gather(key_weight, "passage", axis=0, tiled=True),
        lax.all_gather(value_weight, "passage", axis=0, tiled=True),
    )
    width = key_weight.shape[1]
    heads = width // DH
    key_rows = jnp.dot(normed, full_key, preferred_element_type=jnp.float32).astype(jnp.bfloat16)
    value_rows = jnp.dot(normed, full_value, preferred_element_type=jnp.float32).astype(
        jnp.bfloat16
    )
    key_rows = key_rows.reshape(MOST, LEN, heads, DH)
    value_rows = value_rows.reshape(MOST, LEN, heads, DH)
    all_queries = lax.all_gather(queries, "passage", axis=0, tiled=True)
    query_total = all_queries.shape[0]
    best_score = jnp.full((query_total, heads), -1e30, jnp.float32)
    row_total = jnp.zeros((query_total, heads), jnp.float32)
    context_sum = jnp.zeros((query_total, width), jnp.float32)
    positions = jnp.arange(LEN, dtype=jnp.int32)
    scaling = DH ** (-0.5)
    for number in range(MOST):
        first_row = slot_question[number] * QT
        block = lax.dynamic_slice_in_dim(all_queries, first_row, QT, 0).reshape(QT, heads, DH)
        scores = (
            jnp.einsum("thd,lhd->htl", block, key_rows[number], preferred_element_type=jnp.float32)
            * scaling
        )
        live_mask = (positions < slot_lengths[number])[None, None, :]
        scores = jnp.where(live_mask, scores, jnp.float32(-1e30))
        top_score = jnp.max(scores, axis=-1)
        weights = jnp.where(live_mask, jnp.exp(scores - top_score[..., None]), jnp.float32(0.0))
        row_mass = jnp.sum(weights, axis=-1)
        partial_ctx = jnp.einsum(
            "htl,lhd->thd",
            weights.astype(jnp.bfloat16),
            value_rows[number],
            preferred_element_type=jnp.float32,
        ).reshape(QT, width)
        old_state = (
            lax.dynamic_slice_in_dim(best_score, first_row, QT, 0),
            lax.dynamic_slice_in_dim(row_total, first_row, QT, 0),
            lax.dynamic_slice_in_dim(context_sum, first_row, QT, 0),
        )
        new_top, new_mass, new_ctx = join_partials(
            old_state, (top_score.T, row_mass.T, partial_ctx)
        )
        best_score = lax.dynamic_update_slice_in_dim(best_score, new_top, first_row, 0)
        row_total = lax.dynamic_update_slice_in_dim(row_total, new_mass, first_row, 0)
        context_sum = lax.dynamic_update_slice_in_dim(context_sum, new_ctx, first_row, 0)
    global_top = lax.pmax(best_score, "passage")
    rescale = jnp.exp(best_score - global_top)
    own_mass, own_ctx = (
        lax.psum_scatter(row_total * rescale, "passage", scatter_dimension=0, tiled=True),
        lax.psum_scatter(context_sum * widen(rescale), "passage", scatter_dimension=0, tiled=True),
    )
    return (own_ctx / widen(own_mass)).astype(jnp.bfloat16)


MESH = pl.DeviceIdType.MESH


def reader_kernel(
    ids_ref,
    place_ref,
    count_ref,
    corpus_ref,
    query_ref,
    key_ref,
    value_ref,
    out_ref,
    tokens,
    normed,
    weights,
    query_in,
    query_all,
    query_wide,
    exp_rows,
    stats,
    partial_out,
    partial_in,
    w_send,
    w_recv,
    q_send,
    q_recv,
    s_send,
    s_recv,
    c_send,
    c_recv,
    local_sem,
):
    rows_here, length, width_in = corpus_ref.shape
    shard_rows, width = key_ref.shape
    half = shard_rows // 2
    heads = width // DH
    per_question = ids_ref.shape[1]
    group = lax.axis_index("groups")
    shard = lax.axis_index("passage")
    z = shard // 2
    x = shard % 2
    z1 = z + 1 - 2 * (z % 2)
    z2 = (z + 2) % 4
    z3 = 3 - z
    xo = 1 - x
    go = 1 - group
    at_x = {"passage": z * 2 + xo}
    at_y = {"groups": go}

    barrier = pltpu.get_barrier_semaphore()
    for step in range(1, 8):
        peer = (shard + step) % 8
        pl.semaphore_signal(barrier, inc=1, device_id={"passage": peer}, device_id_type=MESH)
    pl.semaphore_signal(barrier, inc=1, device_id=at_y, device_id_type=MESH)

    corpus_copies = []
    for row in range(rows_here):
        copy = pltpu.make_async_copy(corpus_ref.at[row], tokens.at[row], local_sem.at[row])
        copy.start()
        corpus_copies.append(copy)
    place_copies = []
    for which, ref in ((0, key_ref), (1, value_ref)):
        start = pl.multiple_of(shard * shard_rows, shard_rows)
        copy = pltpu.make_async_copy(
            ref, weights.at[which, pl.ds(start, shard_rows)], local_sem.at[rows_here + which]
        )
        copy.start()
        place_copies.append(copy)
    own_query = pltpu.make_async_copy(
        query_ref, query_in.at[shard], local_sem.at[rows_here + 2]
    )
    own_query.start()
    pl.semaphore_wait(barrier, 8)

    def region(which, zz, xx, part):
        base = (zz * 2 + xx) * shard_rows
        if part is None:
            return weights.at[which, pl.ds(pl.multiple_of(base, shard_rows), shard_rows)]
        return weights.at[which, pl.ds(pl.multiple_of(base + part * half, half), half)]

    def send(which, number, source, target, device):
        copy = pltpu.make_async_remote_copy(
            src_ref=source,
            dst_ref=target,
            send_sem=w_send.at[which, number],
            recv_sem=w_recv.at[which, number],
            device_id=device,
            device_id_type=MESH,
        )
        copy.start()
        sent.append(copy)

    def landed(which, number, target):
        pltpu.make_async_remote_copy(
            src_ref=target,
            dst_ref=target,
            send_sem=w_send.at[which, number],
            recv_sem=w_recv.at[which, number],
            device_id=at_x,
            device_id_type=MESH,
        ).wait_recv()

    sent = []
    for step in range(1, 8):
        peer = (shard + step) % 8
        copy = pltpu.make_async_remote_copy(
            src_ref=query_ref,
            dst_ref=query_in.at[shard],
            send_sem=q_send.at[step],
            recv_sem=q_recv.at[step],
            device_id={"passage": peer},
            device_id_type=MESH,
        )
        copy.start()
        sent.append(copy)

    for which, ref in ((0, key_ref), (1, value_ref)):
        mine = ref.at[pl.ds(pl.multiple_of(group * half, half), half)]
        send(which, 0, ref, region(which, z, x, None), {"passage": z1 * 2 + x})
        send(which, 3, ref, region(which, z, x, None), at_x)
        send(which, 1, mine, region(which, z, x, group), {"passage": z2 * 2 + x})
        send(which, 2, mine, region(which, z, x, group), {"passage": z3 * 2 + x})

    def forward(which, number):
        if number == 0:
            landed(which, 0, region(which, z1, x, None))
            piece = region(which, z1, x, group)
            send(which, 4, piece, piece, at_x)
        elif number in (1, 2):
            zz = (z2, z3)[number - 1]
            piece = region(which, zz, x, group)
            landed(which, number, piece)
            send(which, 4 + number, piece, piece, at_x)
            send(which, 6 + number, piece, piece, at_y)
        else:
            zz = (z1, z2, z3)[number - 4]
            piece = region(which, zz, xo, group)
            landed(which, number, piece)
            send(which, 5 + number, piece, piece, at_y)

    def last_pieces(which):
        landed(which, 3, region(which, z, xo, None))
        landed(which, 7, region(which, z2, x, go))
        landed(which, 8, region(which, z3, x, go))
        landed(which, 9, region(which, z1, xo, go))
        landed(which, 10, region(which, z2, xo, go))
        landed(which, 11, region(which, z3, xo, go))

    def norm(row):
        corpus_copies[row].wait()
        values32 = tokens[row].astype(jnp.float32)
        factor = lax.rsqrt(jnp.mean(values32 * values32, axis=-1, keepdims=True) + 1e-06)
        normed[row] = (values32 * factor).astype(jnp.bfloat16)

    norm(0)
    norm(1)
    forward(0, 0)
    norm(2)
    forward(0, 1)
    forward(0, 2)
    norm(3)
    forward(0, 4)
    forward(1, 0)
    norm(4)
    forward(0, 5)
    forward(0, 6)
    forward(1, 1)
    forward(1, 2)
    norm(5)

    lengths = [jnp.int32(0) for _ in range(rows_here)]
    for number in range(per_question):
        name = ids_ref[0, number]
        place = place_ref[name] - shard * rows_here
        count = count_ref[name]
        lengths = [
            kept + jnp.where(place == row, count, 0) for row, kept in enumerate(lengths)
        ]

    own_query.wait()
    for step in range(1, 8):
        origin = (shard + 8 - step) % 8
        pltpu.make_async_remote_copy(
            src_ref=query_ref,
            dst_ref=query_in.at[origin],
            send_sem=q_send.at[step],
            recv_sem=q_recv.at[step],
            device_id=at_x,
            device_id_type=MESH,
        ).wait_recv()
    for number in range(8):
        query_all[2 * number : 2 * number + 2, :] = query_in[number].astype(jnp.float32)
    block = jnp.concatenate([query_all[...]] * heads, axis=0)
    row_head = lax.broadcasted_iota(jnp.int32, (heads * QT, width), 0) // QT
    col_head = lax.broadcasted_iota(jnp.int32, (heads * QT, width), 1) // DH
    query_wide[...] = jnp.where(row_head == col_head, block, 0.0).astype(jnp.bfloat16)

    forward(1, 4)
    forward(1, 5)
    forward(1, 6)
    place_copies[0].wait()
    last_pieces(0)

    scaling = DH ** (-0.5)
    positions = lax.broadcasted_iota(jnp.int32, (length, heads * QT), 0)
    tops, masses = [], []
    for row in range(rows_here):
        key_rows = jnp.dot(
            normed[row], weights[0], preferred_element_type=jnp.float32
        ).astype(jnp.bfloat16)
        scores = (
            lax.dot_general(
                key_rows,
                query_wide[...],
                (((1,), (1,)), ((), ())),
                preferred_element_type=jnp.float32,
            )
            * scaling
        )
        live = positions < lengths[row]
        scores = jnp.where(live, scores, jnp.float32(-1e30))
        top = jnp.max(scores, axis=0, keepdims=True)
        exps = jnp.where(live, jnp.exp(scores - top), jnp.float32(0.0))
        masses.append(jnp.sum(exps, axis=0, keepdims=True))
        tops.append(top)
        exp_rows[row] = exps.astype(jnp.bfloat16)
    peak_here = tops[0]
    for top in tops[1:]:
        peak_here = jnp.maximum(peak_here, top)
    mass_here = masses[0] * jnp.exp(tops[0] - peak_here)
    for top, mass in zip(tops[1:], masses[1:]):
        mass_here = mass_here + mass * jnp.exp(top - peak_here)
    stats[shard] = jnp.concatenate([peak_here, mass_here], axis=0)
    for step in range(1, 8):
        peer = (shard + step) % 8
        copy = pltpu.make_async_remote_copy(
            src_ref=stats.at[shard],
            dst_ref=stats.at[shard],
            send_sem=s_send.at[step],
            recv_sem=s_recv.at[step],
            device_id={"passage": peer},
            device_id_type=MESH,
        )
        copy.start()
        sent.append(copy)
    for step in range(1, 8):
        origin = (shard + 8 - step) % 8
        pltpu.make_async_remote_copy(
            src_ref=stats.at[origin],
            dst_ref=stats.at[origin],
            send_sem=s_send.at[step],
            recv_sem=s_recv.at[step],
            device_id=at_x,
            device_id_type=MESH,
        ).wait_recv()
    peak = stats[0, 0:1, :]
    for number in range(1, 8):
        peak = jnp.maximum(peak, stats[number, 0:1, :])
    total = jnp.zeros_like(peak)
    for number in range(8):
        total = total + stats[number, 1:2, :] * jnp.exp(stats[number, 0:1, :] - peak)
    factors = [jnp.exp(top - peak) / total for top in tops]
    factors += [jnp.zeros_like(peak)] * (8 - rows_here)
    factors = jnp.transpose(jnp.concatenate(factors, axis=0))
    context = jnp.zeros((heads * QT, width_in), jnp.float32)
    for row in range(rows_here):
        context = context + factors[:, row : row + 1] * lax.dot_general(
            exp_rows[row],
            normed[row],
            (((0,), (0,)), ((), ())),
            preferred_element_type=jnp.float32,
        )
    context = context.astype(jnp.bfloat16)

    place_copies[1].wait()
    last_pieces(1)
    mixed = jnp.dot(context, weights[1], preferred_element_type=jnp.float32)
    mixed = jnp.where(row_head == col_head, mixed, 0.0)
    summed = mixed[0:QT]
    for head in range(1, heads):
        summed = summed + mixed[head * QT : (head + 1) * QT]
    for number in range(8):
        partial_out[number] = summed[2 * number : 2 * number + 2]
    for step in range(1, 8):
        peer = (shard + step) % 8
        copy = pltpu.make_async_remote_copy(
            src_ref=partial_out.at[peer],
            dst_ref=partial_in.at[shard],
            send_sem=c_send.at[step],
            recv_sem=c_recv.at[step],
            device_id={"passage": peer},
            device_id_type=MESH,
        )
        copy.start()
        sent.append(copy)
    result = partial_out[shard]
    for step in range(1, 8):
        origin = (shard + 8 - step) % 8
        pltpu.make_async_remote_copy(
            src_ref=partial_out.at[origin],
            dst_ref=partial_in.at[origin],
            send_sem=c_send.at[step],
            recv_sem=c_recv.at[step],
            device_id=at_x,
            device_id_type=MESH,
        ).wait_recv()
        result = result + partial_in[origin]
    out_ref[...] = result.astype(jnp.bfloat16)
    for copy in sent:
        copy.wait_send()


def one_question(corpus, queries, key_weight, value_weight, retrieved, placement_map, valid_counts):
    rows_here, length, width_in = corpus.shape
    shard_rows, width = key_weight.shape
    lanes = width // DH * QT
    smem = pl.BlockSpec(memory_space=pltpu.SMEM)
    anywhere = pl.BlockSpec(memory_space=pl.ANY)
    vmem = pl.BlockSpec(memory_space=pltpu.VMEM)
    dma = pltpu.SemaphoreType.DMA
    return pl.pallas_call(
        reader_kernel,
        out_shape=jax.ShapeDtypeStruct(queries.shape, jnp.bfloat16),
        in_specs=[smem, smem, smem, anywhere, anywhere, anywhere, anywhere],
        out_specs=vmem,
        scratch_shapes=[
            pltpu.VMEM(corpus.shape, jnp.bfloat16),
            pltpu.VMEM(corpus.shape, jnp.bfloat16),
            pltpu.VMEM((2, 8 * shard_rows, width), jnp.bfloat16),
            pltpu.VMEM((8, 2, width), jnp.bfloat16),
            pltpu.VMEM((QT, width), jnp.float32),
            pltpu.VMEM((lanes, width), jnp.bfloat16),
            pltpu.VMEM((rows_here, length, lanes), jnp.bfloat16),
            pltpu.VMEM((8, 2, lanes), jnp.float32),
            pltpu.VMEM((8, 2, width), jnp.float32),
            pltpu.VMEM((8, 2, width), jnp.float32),
            dma((2, 12)),
            dma((2, 12)),
            dma((8,)),
            dma((8,)),
            dma((8,)),
            dma((8,)),
            dma((8,)),
            dma((8,)),
            dma((rows_here + 3,)),
        ],
        compiler_params=pltpu.CompilerParams(
            collective_id=0, has_side_effects=True, vmem_limit_bytes=48 * 1024 * 1024
        ),
    )(retrieved, placement_map, valid_counts, corpus, queries, key_weight, value_weight)


def route(*args):
    corpus, queries, key_weight, value_weight, retrieved, placement_map, valid_counts = args
    small = (
        lax.axis_size("groups") == 2
        and lax.axis_size("passage") == 8
        and retrieved.shape[0] == 1
        and queries.shape[0] == 2
    )
    return one_question(*args) if small else on_device(*args)


def solution(mesh):
    in_specs = (
        P(("groups", "passage"), None, None),
        P(("groups", "passage"), "tensor"),
        P("passage", "tensor"),
        P("passage", "tensor"),
        P("groups", None),
        P("groups"),
        P("groups"),
    )
    out_specs = P(("groups", "passage"), "tensor")
    return jax.shard_map(
        route, mesh=mesh, in_specs=in_specs, out_specs=out_specs, check_vma=False
    )
```

```python
import jax
import jax.numpy as jnp
from jax import lax
from jax.experimental import pallas as pl
from jax.experimental.pallas import tpu as pltpu
from jax.sharding import PartitionSpec as P

DH = 64
LEN = 256
MOST = 5
QT = 16


def normalize(hidden):
    values32 = hidden.astype(jnp.float32)
    factor = lax.rsqrt(jnp.mean(values32 * values32, axis=-1, keepdims=True) + 1e-06)
    return (values32 * factor).astype(jnp.bfloat16)


def widen(stats):
    return jnp.repeat(stats, DH, axis=-1)


def join_partials(first, second):
    top_one, mass_one, ctx_one = first
    top_two, mass_two, ctx_two = second
    highest = jnp.maximum(top_one, top_two)
    scale_one = jnp.exp(top_one - highest)
    scale_two = jnp.exp(top_two - highest)
    return (
        highest,
        mass_one * scale_one + mass_two * scale_two,
        ctx_one * widen(scale_one) + ctx_two * widen(scale_two),
    )


def on_device(corpus, queries, key_weight, value_weight, retrieved, placement_map, valid_counts):
    shard_index = lax.axis_index("passage")
    corp_rows = corpus.shape[0]
    per_question = retrieved.shape[1]
    total_ret = retrieved.shape[0] * per_question
    flat_ids = retrieved.reshape(total_ret)
    corpus_row = placement_map[flat_ids]
    lengths = valid_counts[flat_ids]
    owned_mask = corpus_row // corp_rows == shard_index
    owner_rank = jnp.cumsum(owned_mask.astype(jnp.int32)) - 1
    slot_iota = jnp.arange(MOST, dtype=jnp.int32)
    selector = (owned_mask[None, :] & (owner_rank[None, :] == slot_iota[:, None])).astype(jnp.int32)
    local_rows = jnp.sum(selector * (corpus_row % corp_rows)[None, :], axis=1)
    slot_lengths = jnp.sum(selector * lengths[None, :], axis=1)
    question_ids = jnp.arange(total_ret, dtype=jnp.int32) // per_question
    slot_question = jnp.sum(selector * question_ids[None, :], axis=1)
    passages = corpus[local_rows]
    normed = normalize(passages).reshape(MOST * LEN, passages.shape[2])
    full_key, full_value = (
        lax.all_gather(key_weight, "passage", axis=0, tiled=True),
        lax.all_gather(value_weight, "passage", axis=0, tiled=True),
    )
    width = key_weight.shape[1]
    heads = width // DH
    key_rows = jnp.dot(normed, full_key, preferred_element_type=jnp.float32).astype(jnp.bfloat16)
    value_rows = jnp.dot(normed, full_value, preferred_element_type=jnp.float32).astype(
        jnp.bfloat16
    )
    key_rows = key_rows.reshape(MOST, LEN, heads, DH)
    value_rows = value_rows.reshape(MOST, LEN, heads, DH)
    all_queries = lax.all_gather(queries, "passage", axis=0, tiled=True)
    query_total = all_queries.shape[0]
    best_score = jnp.full((query_total, heads), -1e30, jnp.float32)
    row_total = jnp.zeros((query_total, heads), jnp.float32)
    context_sum = jnp.zeros((query_total, width), jnp.float32)
    positions = jnp.arange(LEN, dtype=jnp.int32)
    scaling = DH ** (-0.5)
    for number in range(MOST):
        first_row = slot_question[number] * QT
        block = lax.dynamic_slice_in_dim(all_queries, first_row, QT, 0).reshape(QT, heads, DH)
        scores = (
            jnp.einsum("thd,lhd->htl", block, key_rows[number], preferred_element_type=jnp.float32)
            * scaling
        )
        live_mask = (positions < slot_lengths[number])[None, None, :]
        scores = jnp.where(live_mask, scores, jnp.float32(-1e30))
        top_score = jnp.max(scores, axis=-1)
        weights = jnp.where(live_mask, jnp.exp(scores - top_score[..., None]), jnp.float32(0.0))
        row_mass = jnp.sum(weights, axis=-1)
        partial_ctx = jnp.einsum(
            "htl,lhd->thd",
            weights.astype(jnp.bfloat16),
            value_rows[number],
            preferred_element_type=jnp.float32,
        ).reshape(QT, width)
        old_state = (
            lax.dynamic_slice_in_dim(best_score, first_row, QT, 0),
            lax.dynamic_slice_in_dim(row_total, first_row, QT, 0),
            lax.dynamic_slice_in_dim(context_sum, first_row, QT, 0),
        )
        new_top, new_mass, new_ctx = join_partials(
            old_state, (top_score.T, row_mass.T, partial_ctx)
        )
        best_score = lax.dynamic_update_slice_in_dim(best_score, new_top, first_row, 0)
        row_total = lax.dynamic_update_slice_in_dim(row_total, new_mass, first_row, 0)
        context_sum = lax.dynamic_update_slice_in_dim(context_sum, new_ctx, first_row, 0)
    global_top = lax.pmax(best_score, "passage")
    rescale = jnp.exp(best_score - global_top)
    own_mass, own_ctx = (
        lax.psum_scatter(row_total * rescale, "passage", scatter_dimension=0, tiled=True),
        lax.psum_scatter(context_sum * widen(rescale), "passage", scatter_dimension=0, tiled=True),
    )
    return (own_ctx / widen(own_mass)).astype(jnp.bfloat16)


MESH = pl.DeviceIdType.MESH


def reader_kernel(
    ids_in,
    place_in,
    count_in,
    corpus_ref,
    query_ref,
    key_ref,
    value_ref,
    out_ref,
    tokens,
    normed,
    weights,
    query_in,
    query_all,
    query_wide,
    exp_rows,
    stats,
    partial_out,
    partial_in,
    w_send,
    w_recv,
    q_send,
    q_recv,
    s_send,
    s_recv,
    c_send,
    c_recv,
    local_sem,
    ids_ref,
    place_ref,
    count_ref,
):
    rows_here, length, width_in = corpus_ref.shape
    shard_rows, width = key_ref.shape
    half = shard_rows // 2
    heads = width // DH
    per_question = ids_in.shape[1]
    group = lax.axis_index("groups")
    shard = lax.axis_index("passage")
    z = shard // 2
    x = shard % 2
    z1 = z + 1 - 2 * (z % 2)
    z2 = (z + 2) % 4
    z3 = 3 - z
    xo = 1 - x
    go = 1 - group
    at_x = {"passage": z * 2 + xo}
    at_y = {"groups": go}

    barrier = pltpu.get_barrier_semaphore()
    for step in range(1, 8):
        peer = (shard + step) % 8
        pl.semaphore_signal(barrier, inc=1, device_id={"passage": peer}, device_id_type=MESH)
    pl.semaphore_signal(barrier, inc=1, device_id=at_y, device_id_type=MESH)

    corpus_copies = []
    for row in range(rows_here):
        copy = pltpu.make_async_copy(corpus_ref.at[row], tokens.at[row], local_sem.at[row])
        copy.start()
        corpus_copies.append(copy)
    place_copies = []
    for which, ref in ((0, key_ref), (1, value_ref)):
        start = pl.multiple_of(shard * shard_rows, shard_rows)
        copy = pltpu.make_async_copy(
            ref, weights.at[which, pl.ds(start, shard_rows)], local_sem.at[rows_here + which]
        )
        copy.start()
        place_copies.append(copy)
    own_query = pltpu.make_async_copy(
        query_ref, query_in.at[shard], local_sem.at[rows_here + 2]
    )
    own_query.start()
    table_copies = []
    for slot, (table, held) in enumerate(
        ((ids_in, ids_ref), (place_in, place_ref), (count_in, count_ref))
    ):
        copy = pltpu.make_async_copy(table, held, local_sem.at[rows_here + 3 + slot])
        copy.start()
        table_copies.append(copy)
    pl.semaphore_wait(barrier, 8)

    def region(which, zz, xx, part):
        base = (zz * 2 + xx) * shard_rows
        if part is None:
            return weights.at[which, pl.ds(pl.multiple_of(base, shard_rows), shard_rows)]
        return weights.at[which, pl.ds(pl.multiple_of(base + part * half, half), half)]

    def send(which, number, source, target, device):
        copy = pltpu.make_async_remote_copy(
            src_ref=source,
            dst_ref=target,
            send_sem=w_send.at[which, number],
            recv_sem=w_recv.at[which, number],
            device_id=device,
            device_id_type=MESH,
        )
        copy.start()
        sent.append(copy)

    def landed(which, number, target):
        pltpu.make_async_remote_copy(
            src_ref=target,
            dst_ref=target,
            send_sem=w_send.at[which, number],
            recv_sem=w_recv.at[which, number],
            device_id=at_x,
            device_id_type=MESH,
        ).wait_recv()

    sent = []
    for step in range(1, 8):
        peer = (shard + step) % 8
        copy = pltpu.make_async_remote_copy(
            src_ref=query_ref,
            dst_ref=query_in.at[shard],
            send_sem=q_send.at[step],
            recv_sem=q_recv.at[step],
            device_id={"passage": peer},
            device_id_type=MESH,
        )
        copy.start()
        sent.append(copy)

    for which, ref in ((0, key_ref), (1, value_ref)):
        mine = ref.at[pl.ds(pl.multiple_of(group * half, half), half)]
        send(which, 0, ref, region(which, z, x, None), {"passage": z1 * 2 + x})
        send(which, 3, ref, region(which, z, x, None), at_x)
        send(which, 1, mine, region(which, z, x, group), {"passage": z2 * 2 + x})
        send(which, 2, mine, region(which, z, x, group), {"passage": z3 * 2 + x})

    def forward(which, number):
        if number == 0:
            landed(which, 0, region(which, z1, x, None))
            piece = region(which, z1, x, group)
            send(which, 4, piece, piece, at_x)
        elif number in (1, 2):
            zz = (z2, z3)[number - 1]
            piece = region(which, zz, x, group)
            landed(which, number, piece)
            send(which, 4 + number, piece, piece, at_x)
            send(which, 6 + number, piece, piece, at_y)
        else:
            zz = (z1, z2, z3)[number - 4]
            piece = region(which, zz, xo, group)
            landed(which, number, piece)
            send(which, 5 + number, piece, piece, at_y)

    def last_pieces(which):
        landed(which, 3, region(which, z, xo, None))
        landed(which, 7, region(which, z2, x, go))
        landed(which, 8, region(which, z3, x, go))
        landed(which, 9, region(which, z1, xo, go))
        landed(which, 10, region(which, z2, xo, go))
        landed(which, 11, region(which, z3, xo, go))

    def norm(row):
        corpus_copies[row].wait()
        values32 = tokens[row].astype(jnp.float32)
        factor = lax.rsqrt(jnp.mean(values32 * values32, axis=-1, keepdims=True) + 1e-06)
        normed[row] = (values32 * factor).astype(jnp.bfloat16)

    norm(0)
    norm(1)
    forward(0, 0)
    norm(2)
    forward(0, 1)
    forward(0, 2)
    norm(3)
    forward(0, 4)
    forward(1, 0)
    norm(4)
    forward(0, 5)
    forward(0, 6)
    forward(1, 1)
    forward(1, 2)
    norm(5)

    for copy in table_copies:
        copy.wait()
    lengths = [jnp.int32(0) for _ in range(rows_here)]
    for number in range(per_question):
        name = ids_ref[0, number]
        place = place_ref[name] - shard * rows_here
        count = count_ref[name]
        lengths = [
            kept + jnp.where(place == row, count, 0) for row, kept in enumerate(lengths)
        ]

    own_query.wait()
    for step in range(1, 8):
        origin = (shard + 8 - step) % 8
        pltpu.make_async_remote_copy(
            src_ref=query_ref,
            dst_ref=query_in.at[origin],
            send_sem=q_send.at[step],
            recv_sem=q_recv.at[step],
            device_id=at_x,
            device_id_type=MESH,
        ).wait_recv()
    for number in range(8):
        query_all[2 * number : 2 * number + 2, :] = query_in[number].astype(jnp.float32)
    block = jnp.concatenate([query_all[...]] * heads, axis=0)
    row_head = lax.broadcasted_iota(jnp.int32, (heads * QT, width), 0) // QT
    col_head = lax.broadcasted_iota(jnp.int32, (heads * QT, width), 1) // DH
    query_wide[...] = jnp.where(row_head == col_head, block, 0.0).astype(jnp.bfloat16)

    forward(1, 4)
    forward(1, 5)
    forward(1, 6)
    place_copies[0].wait()
    last_pieces(0)

    scaling = DH ** (-0.5)
    positions = lax.broadcasted_iota(jnp.int32, (length, heads * QT), 0)
    tops, masses = [], []
    for row in range(rows_here):
        key_rows = jnp.dot(
            normed[row], weights[0], preferred_element_type=jnp.float32
        ).astype(jnp.bfloat16)
        scores = (
            lax.dot_general(
                key_rows,
                query_wide[...],
                (((1,), (1,)), ((), ())),
                preferred_element_type=jnp.float32,
            )
            * scaling
        )
        live = positions < lengths[row]
        scores = jnp.where(live, scores, jnp.float32(-1e30))
        top = jnp.max(scores, axis=0, keepdims=True)
        exps = jnp.where(live, jnp.exp(scores - top), jnp.float32(0.0))
        masses.append(jnp.sum(exps, axis=0, keepdims=True))
        tops.append(top)
        exp_rows[row] = exps.astype(jnp.bfloat16)
    peak_here = tops[0]
    for top in tops[1:]:
        peak_here = jnp.maximum(peak_here, top)
    mass_here = masses[0] * jnp.exp(tops[0] - peak_here)
    for top, mass in zip(tops[1:], masses[1:]):
        mass_here = mass_here + mass * jnp.exp(top - peak_here)
    stats[shard] = jnp.concatenate([peak_here, mass_here], axis=0)
    for step in range(1, 8):
        peer = (shard + step) % 8
        copy = pltpu.make_async_remote_copy(
            src_ref=stats.at[shard],
            dst_ref=stats.at[shard],
            send_sem=s_send.at[step],
            recv_sem=s_recv.at[step],
            device_id={"passage": peer},
            device_id_type=MESH,
        )
        copy.start()
        sent.append(copy)
    for step in range(1, 8):
        origin = (shard + 8 - step) % 8
        pltpu.make_async_remote_copy(
            src_ref=stats.at[origin],
            dst_ref=stats.at[origin],
            send_sem=s_send.at[step],
            recv_sem=s_recv.at[step],
            device_id=at_x,
            device_id_type=MESH,
        ).wait_recv()
    peak = stats[0, 0:1, :]
    for number in range(1, 8):
        peak = jnp.maximum(peak, stats[number, 0:1, :])
    total = jnp.zeros_like(peak)
    for number in range(8):
        total = total + stats[number, 1:2, :] * jnp.exp(stats[number, 0:1, :] - peak)
    factors = [jnp.exp(top - peak) / total for top in tops]
    factors += [jnp.zeros_like(peak)] * (8 - rows_here)
    factors = jnp.transpose(jnp.concatenate(factors, axis=0))
    context = jnp.zeros((heads * QT, width_in), jnp.float32)
    for row in range(rows_here):
        context = context + factors[:, row : row + 1] * lax.dot_general(
            exp_rows[row],
            normed[row],
            (((0,), (0,)), ((), ())),
            preferred_element_type=jnp.float32,
        )
    context = context.astype(jnp.bfloat16)

    place_copies[1].wait()
    last_pieces(1)
    mixed = jnp.dot(context, weights[1], preferred_element_type=jnp.float32)
    mixed = jnp.where(row_head == col_head, mixed, 0.0)
    summed = mixed[0:QT]
    for head in range(1, heads):
        summed = summed + mixed[head * QT : (head + 1) * QT]
    for number in range(8):
        partial_out[number] = summed[2 * number : 2 * number + 2]
    for step in range(1, 8):
        peer = (shard + step) % 8
        copy = pltpu.make_async_remote_copy(
            src_ref=partial_out.at[peer],
            dst_ref=partial_in.at[shard],
            send_sem=c_send.at[step],
            recv_sem=c_recv.at[step],
            device_id={"passage": peer},
            device_id_type=MESH,
        )
        copy.start()
        sent.append(copy)
    result = partial_out[shard]
    for step in range(1, 8):
        origin = (shard + 8 - step) % 8
        pltpu.make_async_remote_copy(
            src_ref=partial_out.at[origin],
            dst_ref=partial_in.at[origin],
            send_sem=c_send.at[step],
            recv_sem=c_recv.at[step],
            device_id=at_x,
            device_id_type=MESH,
        ).wait_recv()
        result = result + partial_in[origin]
    out_ref[...] = result.astype(jnp.bfloat16)
    for copy in sent:
        copy.wait_send()


def one_question(corpus, queries, key_weight, value_weight, retrieved, placement_map, valid_counts):
    rows_here, length, width_in = corpus.shape
    shard_rows, width = key_weight.shape
    lanes = width // DH * QT
    hbm = pl.BlockSpec(memory_space=pltpu.HBM)
    vmem = pl.BlockSpec(memory_space=pltpu.VMEM)
    dma = pltpu.SemaphoreType.DMA
    return pl.pallas_call(
        reader_kernel,
        out_shape=jax.ShapeDtypeStruct(queries.shape, jnp.bfloat16),
        in_specs=[hbm] * 7,
        out_specs=vmem,
        scratch_shapes=[
            pltpu.VMEM(corpus.shape, jnp.bfloat16),
            pltpu.VMEM(corpus.shape, jnp.bfloat16),
            pltpu.VMEM((2, 8 * shard_rows, width), jnp.bfloat16),
            pltpu.VMEM((8, 2, width), jnp.bfloat16),
            pltpu.VMEM((QT, width), jnp.float32),
            pltpu.VMEM((lanes, width), jnp.bfloat16),
            pltpu.VMEM((rows_here, length, lanes), jnp.bfloat16),
            pltpu.VMEM((8, 2, lanes), jnp.float32),
            pltpu.VMEM((8, 2, width), jnp.float32),
            pltpu.VMEM((8, 2, width), jnp.float32),
            dma((2, 12)),
            dma((2, 12)),
            dma((8,)),
            dma((8,)),
            dma((8,)),
            dma((8,)),
            dma((8,)),
            dma((8,)),
            dma((rows_here + 6,)),
            pltpu.SMEM(retrieved.shape, jnp.int32),
            pltpu.SMEM(placement_map.shape, jnp.int32),
            pltpu.SMEM(valid_counts.shape, jnp.int32),
        ],
        compiler_params=pltpu.CompilerParams(
            collective_id=0, has_side_effects=True, vmem_limit_bytes=60 * 1024 * 1024
        ),
    )(retrieved, placement_map, valid_counts, corpus, queries, key_weight, value_weight)


def route(*args):
    corpus, queries, key_weight, value_weight, retrieved, placement_map, valid_counts = args
    small = (
        lax.axis_size("groups") == 2
        and lax.axis_size("passage") == 8
        and retrieved.shape[0] == 1
        and queries.shape[0] == 2
    )
    return one_question(*args) if small else on_device(*args)


def solution(mesh):
    in_specs = (
        P(("groups", "passage"), None, None),
        P(("groups", "passage"), "tensor"),
        P("passage", "tensor"),
        P("passage", "tensor"),
        P("groups", None),
        P("groups"),
        P("groups"),
    )
    out_specs = P(("groups", "passage"), "tensor")
    return jax.shard_map(
        route, mesh=mesh, in_specs=in_specs, out_specs=out_specs, check_vma=False
    )
```

```python
import jax
import jax.numpy as jnp
from jax import lax
from jax.experimental import pallas as pl
from jax.experimental.pallas import tpu as pltpu
from jax.sharding import PartitionSpec as P

DH = 64
LEN = 256
MOST = 5
QT = 16


def normalize(hidden):
    values32 = hidden.astype(jnp.float32)
    factor = lax.rsqrt(jnp.mean(values32 * values32, axis=-1, keepdims=True) + 1e-06)
    return (values32 * factor).astype(jnp.bfloat16)


def widen(stats):
    return jnp.repeat(stats, DH, axis=-1)


def join_partials(first, second):
    top_one, mass_one, ctx_one = first
    top_two, mass_two, ctx_two = second
    highest = jnp.maximum(top_one, top_two)
    scale_one = jnp.exp(top_one - highest)
    scale_two = jnp.exp(top_two - highest)
    return (
        highest,
        mass_one * scale_one + mass_two * scale_two,
        ctx_one * widen(scale_one) + ctx_two * widen(scale_two),
    )


def on_device(corpus, queries, key_weight, value_weight, retrieved, placement_map, valid_counts):
    shard_index = lax.axis_index("passage")
    corp_rows = corpus.shape[0]
    per_question = retrieved.shape[1]
    total_ret = retrieved.shape[0] * per_question
    flat_ids = retrieved.reshape(total_ret)
    corpus_row = placement_map[flat_ids]
    lengths = valid_counts[flat_ids]
    owned_mask = corpus_row // corp_rows == shard_index
    owner_rank = jnp.cumsum(owned_mask.astype(jnp.int32)) - 1
    slot_iota = jnp.arange(MOST, dtype=jnp.int32)
    selector = (owned_mask[None, :] & (owner_rank[None, :] == slot_iota[:, None])).astype(jnp.int32)
    local_rows = jnp.sum(selector * (corpus_row % corp_rows)[None, :], axis=1)
    slot_lengths = jnp.sum(selector * lengths[None, :], axis=1)
    question_ids = jnp.arange(total_ret, dtype=jnp.int32) // per_question
    slot_question = jnp.sum(selector * question_ids[None, :], axis=1)
    passages = corpus[local_rows]
    normed = normalize(passages).reshape(MOST * LEN, passages.shape[2])
    full_key, full_value = (
        lax.all_gather(key_weight, "passage", axis=0, tiled=True),
        lax.all_gather(value_weight, "passage", axis=0, tiled=True),
    )
    width = key_weight.shape[1]
    heads = width // DH
    key_rows = jnp.dot(normed, full_key, preferred_element_type=jnp.float32).astype(jnp.bfloat16)
    value_rows = jnp.dot(normed, full_value, preferred_element_type=jnp.float32).astype(
        jnp.bfloat16
    )
    key_rows = key_rows.reshape(MOST, LEN, heads, DH)
    value_rows = value_rows.reshape(MOST, LEN, heads, DH)
    all_queries = lax.all_gather(queries, "passage", axis=0, tiled=True)
    query_total = all_queries.shape[0]
    best_score = jnp.full((query_total, heads), -1e30, jnp.float32)
    row_total = jnp.zeros((query_total, heads), jnp.float32)
    context_sum = jnp.zeros((query_total, width), jnp.float32)
    positions = jnp.arange(LEN, dtype=jnp.int32)
    scaling = DH ** (-0.5)
    for number in range(MOST):
        first_row = slot_question[number] * QT
        block = lax.dynamic_slice_in_dim(all_queries, first_row, QT, 0).reshape(QT, heads, DH)
        scores = (
            jnp.einsum("thd,lhd->htl", block, key_rows[number], preferred_element_type=jnp.float32)
            * scaling
        )
        live_mask = (positions < slot_lengths[number])[None, None, :]
        scores = jnp.where(live_mask, scores, jnp.float32(-1e30))
        top_score = jnp.max(scores, axis=-1)
        weights = jnp.where(live_mask, jnp.exp(scores - top_score[..., None]), jnp.float32(0.0))
        row_mass = jnp.sum(weights, axis=-1)
        partial_ctx = jnp.einsum(
            "htl,lhd->thd",
            weights.astype(jnp.bfloat16),
            value_rows[number],
            preferred_element_type=jnp.float32,
        ).reshape(QT, width)
        old_state = (
            lax.dynamic_slice_in_dim(best_score, first_row, QT, 0),
            lax.dynamic_slice_in_dim(row_total, first_row, QT, 0),
            lax.dynamic_slice_in_dim(context_sum, first_row, QT, 0),
        )
        new_top, new_mass, new_ctx = join_partials(
            old_state, (top_score.T, row_mass.T, partial_ctx)
        )
        best_score = lax.dynamic_update_slice_in_dim(best_score, new_top, first_row, 0)
        row_total = lax.dynamic_update_slice_in_dim(row_total, new_mass, first_row, 0)
        context_sum = lax.dynamic_update_slice_in_dim(context_sum, new_ctx, first_row, 0)
    global_top = lax.pmax(best_score, "passage")
    rescale = jnp.exp(best_score - global_top)
    own_mass, own_ctx = (
        lax.psum_scatter(row_total * rescale, "passage", scatter_dimension=0, tiled=True),
        lax.psum_scatter(context_sum * widen(rescale), "passage", scatter_dimension=0, tiled=True),
    )
    return (own_ctx / widen(own_mass)).astype(jnp.bfloat16)


MESH = pl.DeviceIdType.MESH


def reader_kernel(
    ids_in,
    place_in,
    count_in,
    corpus_ref,
    query_ref,
    key_ref,
    value_ref,
    out_ref,
    tokens,
    normed,
    weights,
    query_in,
    query_all,
    query_wide,
    exp_rows,
    stats,
    partial_out,
    partial_in,
    w_send,
    w_recv,
    q_send,
    q_recv,
    s_send,
    s_recv,
    c_send,
    c_recv,
    local_sem,
    ids_ref,
    place_ref,
    count_ref,
):
    rows_here, length, width_in = corpus_ref.shape
    shard_rows, width = key_ref.shape
    half = shard_rows // 2
    heads = width // DH
    per_question = ids_in.shape[1]
    group = lax.axis_index("groups")
    shard = lax.axis_index("passage")
    z = shard // 2
    x = shard % 2
    z1 = z + 1 - 2 * (z % 2)
    z2 = (z + 2) % 4
    z3 = 3 - z
    xo = 1 - x
    go = 1 - group
    at_x = {"passage": z * 2 + xo}
    at_y = {"groups": go}

    barrier = pltpu.get_barrier_semaphore()
    for step in range(1, 8):
        peer = (shard + step) % 8
        pl.semaphore_signal(barrier, inc=1, device_id={"passage": peer}, device_id_type=MESH)
    pl.semaphore_signal(barrier, inc=1, device_id=at_y, device_id_type=MESH)

    corpus_copies = []
    for row in range(rows_here):
        copy = pltpu.make_async_copy(corpus_ref.at[row], tokens.at[row], local_sem.at[row])
        copy.start()
        corpus_copies.append(copy)
    place_copies = []
    for which, ref in ((0, key_ref), (1, value_ref)):
        start = pl.multiple_of(shard * shard_rows, shard_rows)
        copy = pltpu.make_async_copy(
            ref, weights.at[which, pl.ds(start, shard_rows)], local_sem.at[rows_here + which]
        )
        copy.start()
        place_copies.append(copy)
    own_query = pltpu.make_async_copy(
        query_ref, query_in.at[shard], local_sem.at[rows_here + 2]
    )
    own_query.start()
    table_copies = []
    for slot, (table, held) in enumerate(
        ((ids_in, ids_ref), (place_in, place_ref), (count_in, count_ref))
    ):
        copy = pltpu.make_async_copy(table, held, local_sem.at[rows_here + 3 + slot])
        copy.start()
        table_copies.append(copy)
    pl.semaphore_wait(barrier, 8)

    def region(which, zz, xx, part):
        base = (zz * 2 + xx) * shard_rows
        if part is None:
            return weights.at[which, pl.ds(pl.multiple_of(base, shard_rows), shard_rows)]
        return weights.at[which, pl.ds(pl.multiple_of(base + part * half, half), half)]

    def send(which, number, source, target, device):
        copy = pltpu.make_async_remote_copy(
            src_ref=source,
            dst_ref=target,
            send_sem=w_send.at[which, number],
            recv_sem=w_recv.at[which, number],
            device_id=device,
            device_id_type=MESH,
        )
        copy.start()
        sent.append(copy)

    def landed(which, number, target):
        pltpu.make_async_remote_copy(
            src_ref=target,
            dst_ref=target,
            send_sem=w_send.at[which, number],
            recv_sem=w_recv.at[which, number],
            device_id=at_x,
            device_id_type=MESH,
        ).wait_recv()

    sent = []
    for which, ref in ((0, key_ref), (1, value_ref)):
        mine = ref.at[pl.ds(pl.multiple_of(group * half, half), half)]
        send(which, 0, ref, region(which, z, x, None), {"passage": z1 * 2 + x})
        send(which, 3, ref, region(which, z, x, None), at_x)
        send(which, 1, mine, region(which, z, x, group), {"passage": z2 * 2 + x})
        send(which, 2, mine, region(which, z, x, group), {"passage": z3 * 2 + x})

    for step in range(1, 8):
        peer = (shard + step) % 8
        copy = pltpu.make_async_remote_copy(
            src_ref=query_ref,
            dst_ref=query_in.at[shard],
            send_sem=q_send.at[step],
            recv_sem=q_recv.at[step],
            device_id={"passage": peer},
            device_id_type=MESH,
        )
        copy.start()
        sent.append(copy)

    def forward(which, number):
        if number == 0:
            landed(which, 0, region(which, z1, x, None))
            piece = region(which, z1, x, group)
            send(which, 4, piece, piece, at_x)
        elif number in (1, 2):
            zz = (z2, z3)[number - 1]
            piece = region(which, zz, x, group)
            landed(which, number, piece)
            send(which, 4 + number, piece, piece, at_x)
            send(which, 6 + number, piece, piece, at_y)
        else:
            zz = (z1, z2, z3)[number - 4]
            piece = region(which, zz, xo, group)
            landed(which, number, piece)
            send(which, 5 + number, piece, piece, at_y)

    def last_pieces(which):
        landed(which, 3, region(which, z, xo, None))
        landed(which, 7, region(which, z2, x, go))
        landed(which, 8, region(which, z3, x, go))
        landed(which, 9, region(which, z1, xo, go))
        landed(which, 10, region(which, z2, xo, go))
        landed(which, 11, region(which, z3, xo, go))

    def norm(row):
        corpus_copies[row].wait()
        values32 = tokens[row].astype(jnp.float32)
        factor = lax.rsqrt(jnp.mean(values32 * values32, axis=-1, keepdims=True) + 1e-06)
        normed[row] = (values32 * factor).astype(jnp.bfloat16)

    norm(0)
    norm(1)
    forward(0, 0)
    norm(2)
    forward(0, 1)
    forward(0, 2)
    norm(3)
    forward(0, 4)
    forward(1, 0)
    norm(4)
    forward(0, 5)
    forward(0, 6)
    forward(1, 1)
    forward(1, 2)
    norm(5)

    for copy in table_copies:
        copy.wait()
    lengths = [jnp.int32(0) for _ in range(rows_here)]
    for number in range(per_question):
        name = ids_ref[0, number]
        place = place_ref[name] - shard * rows_here
        count = count_ref[name]
        lengths = [
            kept + jnp.where(place == row, count, 0) for row, kept in enumerate(lengths)
        ]

    own_query.wait()
    for step in range(1, 8):
        origin = (shard + 8 - step) % 8
        pltpu.make_async_remote_copy(
            src_ref=query_ref,
            dst_ref=query_in.at[origin],
            send_sem=q_send.at[step],
            recv_sem=q_recv.at[step],
            device_id=at_x,
            device_id_type=MESH,
        ).wait_recv()
    for number in range(8):
        query_all[2 * number : 2 * number + 2, :] = query_in[number].astype(jnp.float32)
    block = jnp.concatenate([query_all[...]] * heads, axis=0)
    row_head = lax.broadcasted_iota(jnp.int32, (heads * QT, width), 0) // QT
    col_head = lax.broadcasted_iota(jnp.int32, (heads * QT, width), 1) // DH
    query_wide[...] = jnp.where(row_head == col_head, block, 0.0).astype(jnp.bfloat16)

    forward(1, 4)
    forward(1, 5)
    forward(1, 6)
    place_copies[0].wait()
    last_pieces(0)

    scaling = DH ** (-0.5)
    positions = lax.broadcasted_iota(jnp.int32, (length, heads * QT), 0)
    tops, masses = [], []
    for row in range(rows_here):
        key_rows = jnp.dot(
            normed[row], weights[0], preferred_element_type=jnp.float32
        ).astype(jnp.bfloat16)
        scores = (
            lax.dot_general(
                key_rows,
                query_wide[...],
                (((1,), (1,)), ((), ())),
                preferred_element_type=jnp.float32,
            )
            * scaling
        )
        live = positions < lengths[row]
        scores = jnp.where(live, scores, jnp.float32(-1e30))
        top = jnp.max(scores, axis=0, keepdims=True)
        exps = jnp.where(live, jnp.exp(scores - top), jnp.float32(0.0))
        masses.append(jnp.sum(exps, axis=0, keepdims=True))
        tops.append(top)
        exp_rows[row] = exps.astype(jnp.bfloat16)
    peak_here = tops[0]
    for top in tops[1:]:
        peak_here = jnp.maximum(peak_here, top)
    mass_here = masses[0] * jnp.exp(tops[0] - peak_here)
    for top, mass in zip(tops[1:], masses[1:]):
        mass_here = mass_here + mass * jnp.exp(top - peak_here)
    stats[shard] = jnp.concatenate([peak_here, mass_here], axis=0)
    for step in range(1, 8):
        peer = (shard + step) % 8
        copy = pltpu.make_async_remote_copy(
            src_ref=stats.at[shard],
            dst_ref=stats.at[shard],
            send_sem=s_send.at[step],
            recv_sem=s_recv.at[step],
            device_id={"passage": peer},
            device_id_type=MESH,
        )
        copy.start()
        sent.append(copy)
    for step in range(1, 8):
        origin = (shard + 8 - step) % 8
        pltpu.make_async_remote_copy(
            src_ref=stats.at[origin],
            dst_ref=stats.at[origin],
            send_sem=s_send.at[step],
            recv_sem=s_recv.at[step],
            device_id=at_x,
            device_id_type=MESH,
        ).wait_recv()
    peak = stats[0, 0:1, :]
    for number in range(1, 8):
        peak = jnp.maximum(peak, stats[number, 0:1, :])
    total = jnp.zeros_like(peak)
    for number in range(8):
        total = total + stats[number, 1:2, :] * jnp.exp(stats[number, 0:1, :] - peak)
    factors = [jnp.exp(top - peak) / total for top in tops]
    factors += [jnp.zeros_like(peak)] * (8 - rows_here)
    factors = jnp.transpose(jnp.concatenate(factors, axis=0))
    context = jnp.zeros((heads * QT, width_in), jnp.float32)
    for row in range(rows_here):
        context = context + factors[:, row : row + 1] * lax.dot_general(
            exp_rows[row],
            normed[row],
            (((0,), (0,)), ((), ())),
            preferred_element_type=jnp.float32,
        )
    context = context.astype(jnp.bfloat16)

    place_copies[1].wait()
    last_pieces(1)
    mixed = jnp.dot(context, weights[1], preferred_element_type=jnp.float32)
    mixed = jnp.where(row_head == col_head, mixed, 0.0)
    summed = mixed[0:QT]
    for head in range(1, heads):
        summed = summed + mixed[head * QT : (head + 1) * QT]
    for number in range(8):
        partial_out[number] = summed[2 * number : 2 * number + 2]
    for step in range(1, 8):
        peer = (shard + step) % 8
        copy = pltpu.make_async_remote_copy(
            src_ref=partial_out.at[peer],
            dst_ref=partial_in.at[shard],
            send_sem=c_send.at[step],
            recv_sem=c_recv.at[step],
            device_id={"passage": peer},
            device_id_type=MESH,
        )
        copy.start()
        sent.append(copy)
    result = partial_out[shard]
    for step in range(1, 8):
        origin = (shard + 8 - step) % 8
        pltpu.make_async_remote_copy(
            src_ref=partial_out.at[origin],
            dst_ref=partial_in.at[origin],
            send_sem=c_send.at[step],
            recv_sem=c_recv.at[step],
            device_id=at_x,
            device_id_type=MESH,
        ).wait_recv()
        result = result + partial_in[origin]
    out_ref[...] = result.astype(jnp.bfloat16)
    for copy in sent:
        copy.wait_send()


def one_question(corpus, queries, key_weight, value_weight, retrieved, placement_map, valid_counts):
    rows_here, length, width_in = corpus.shape
    shard_rows, width = key_weight.shape
    lanes = width // DH * QT
    hbm = pl.BlockSpec(memory_space=pltpu.HBM)
    vmem = pl.BlockSpec(memory_space=pltpu.VMEM)
    dma = pltpu.SemaphoreType.DMA
    return pl.pallas_call(
        reader_kernel,
        out_shape=jax.ShapeDtypeStruct(queries.shape, jnp.bfloat16),
        in_specs=[hbm] * 7,
        out_specs=vmem,
        scratch_shapes=[
            pltpu.VMEM(corpus.shape, jnp.bfloat16),
            pltpu.VMEM(corpus.shape, jnp.bfloat16),
            pltpu.VMEM((2, 8 * shard_rows, width), jnp.bfloat16),
            pltpu.VMEM((8, 2, width), jnp.bfloat16),
            pltpu.VMEM((QT, width), jnp.float32),
            pltpu.VMEM((lanes, width), jnp.bfloat16),
            pltpu.VMEM((rows_here, length, lanes), jnp.bfloat16),
            pltpu.VMEM((8, 2, lanes), jnp.float32),
            pltpu.VMEM((8, 2, width), jnp.float32),
            pltpu.VMEM((8, 2, width), jnp.float32),
            dma((2, 12)),
            dma((2, 12)),
            dma((8,)),
            dma((8,)),
            dma((8,)),
            dma((8,)),
            dma((8,)),
            dma((8,)),
            dma((rows_here + 6,)),
            pltpu.SMEM(retrieved.shape, jnp.int32),
            pltpu.SMEM(placement_map.shape, jnp.int32),
            pltpu.SMEM(valid_counts.shape, jnp.int32),
        ],
        compiler_params=pltpu.CompilerParams(
            collective_id=0, has_side_effects=True, vmem_limit_bytes=60 * 1024 * 1024
        ),
    )(retrieved, placement_map, valid_counts, corpus, queries, key_weight, value_weight)


def route(*args):
    corpus, queries, key_weight, value_weight, retrieved, placement_map, valid_counts = args
    small = (
        lax.axis_size("groups") == 2
        and lax.axis_size("passage") == 8
        and retrieved.shape[0] == 1
        and queries.shape[0] == 2
    )
    return one_question(*args) if small else on_device(*args)


def solution(mesh):
    in_specs = (
        P(("groups", "passage"), None, None),
        P(("groups", "passage"), "tensor"),
        P("passage", "tensor"),
        P("passage", "tensor"),
        P("groups", None),
        P("groups"),
        P("groups"),
    )
    out_specs = P(("groups", "passage"), "tensor")
    return jax.shard_map(
        route, mesh=mesh, in_specs=in_specs, out_specs=out_specs, check_vma=False
    )
```
